256 devices in a mesh: sec: 4 (over y_lo, core), mom: 8 (over x, y_hi), en: 8 (over z).
Axes of the slice: x: 4, y: 4 (y_hi: 2, y_lo: 2; y = y_hi * 2 + y_lo), z: 8, core: 2. Of those that a mesh axis runs over, the one named last changes fastest.
Arguments:
- green_blocks: bfloat16 [8, 64, 2, 128, 128], P('mom', ('sec', 'en')), may hold values from -6 to 6
- derivative: bfloat16 [3, 128, 128], replicated, may hold values from -0.5 to 0.5
- bare_phonon: float32 [4, 8, 2, 3, 3, 128], P('sec', 'mom'), may hold values from -4 to 4
- prior_polar: float32 [4, 8, 2, 3, 3, 128], P('sec', 'mom'), may hold values from -4 to 4
- offsets: int32 [4], replicated, may hold values from 1 to 2, as said below
- momenta: int32 [8, 8], replicated, may hold values from 0 to 7, as said below
Outputs:
- sigma: float32 [8, 64, 2, 128, 128], P('mom', ('sec', 'en'))
- polarization: float32 [4, 8, 3, 128], P('sec', 'mom')
The draws below stay inside these ranges and needn't reach their ends.
Inputs may be any that keep to these rules, and one draw needn't show every extreme that they name: `offsets`: every mode's offset lies in 1 to 2; some mode's offset equals 2 and another mode's equals 1. momenta[k, k'] = p((k - k') mod 8) for a permutation p of the 8 phonon momenta.
All inputs are finite; a program needn't handle non-finite values.
Results may differ from the reference program's by a relative error of at most 0.014.
Values may be sent and summed in bfloat16 or wider, within the bound.
No kernel may reach another device: no remote copies, remote signals or barrier semaphores. Data moves between devices by JAX's collectives and lax.ppermute only.
A program may use at most 64 MiB of HBM per device.

```python
import math
import jax
import jax.numpy as jnp
from jax import lax

NB = 128
E_DEV = 2
NK = 8
NE = 64
NW = 4


def draw_offsets(key, part):
    base_key = jax.random.fold_in(key, 9173)
    first_key = jax.random.fold_in(base_key, 1)
    second_key = jax.random.fold_in(base_key, 2)
    third_key = jax.random.fold_in(base_key, 3)
    rotation = jax.random.randint(first_key, (), 0, E_DEV)
    extra = jax.random.randint(third_key, (NW,), 0, E_DEV)
    mode_ids = jnp.arange(NW)
    values = 1 + (mode_ids + rotation + extra) % E_DEV
    order = jax.random.permutation(second_key, NW)
    values = jnp.where(mode_ids == order[0], E_DEV, values)
    values = jnp.where(mode_ids == order[1], 1, values)
    return values.astype(jnp.int32)


def draw_momenta(key, part):
    labels = jax.random.permutation(jax.random.fold_in(key, 23), NK).astype(jnp.int32)
    row_ids = jnp.arange(NK, dtype=jnp.int32)[:, None]
    col_ids = jnp.arange(NK, dtype=jnp.int32)[None, :]
    return labels[(row_ids - col_ids) % NK].astype(jnp.int32)


def block_scale(stream_key, shape, pieces, smallest, largest):
    factor_of = 1.0
    for axis_at, shards_of in pieces:
        steps = jax.random.uniform(jax.random.fold_in(jax.random.fold_in(stream_key, 6), axis_at), (shards_of,), jnp.float32, smallest / len(pieces), largest / len(pieces))
        factor_of = factor_of * jnp.repeat(jnp.exp(steps), shape[axis_at] // shards_of).reshape((-1,) + (1,) * (len(shape) - 1 - axis_at))
    return factor_of


def gaussian(own_key, extent, deviation, most, pieces=(), held_as=jnp.bfloat16):
    drawn = deviation * jax.random.normal(own_key, extent, jnp.float32)
    if pieces:
        drawn = drawn * block_scale(own_key, extent, pieces, -0.22, 0.18)
    return jnp.clip(drawn, -most, most).astype(held_as)


def setup_inputs(seed: int = 0) -> dict:
    seeds = jax.random.split(jax.random.key(seed), 7)
    return {
        "green_blocks": gaussian(seeds[0], (NK, NE, 2, NB, NB), 1.0, 6.0, ((0, 8), (1, 32))),
        "derivative": gaussian(seeds[1], (3, NB, NB), NB ** -0.5, 0.5),
        "bare_phonon": gaussian(seeds[2], (NW, NK, 2, 3, 3, NB), 0.5, 4.0, ((0, 4), (1, 8)), jnp.float32),
        "prior_polar": gaussian(seeds[3], (NW, NK, 2, 3, 3, NB), 0.5, 4.0, ((0, 4), (1, 8)), jnp.float32),
        "offsets": draw_offsets(jax.random.fold_in(seeds[6], 71), 0),
        "momenta": draw_momenta(jax.random.fold_in(seeds[6], 71), 0),
    }


def contract(former, latter):
    return lax.optimization_barrier(jnp.sum(former[..., :, :, None, :] * latter[..., None, :, :, :], axis=-3))

def complex_product(former, latter):
    real_part = contract(former[..., 0, :, :, :], latter[..., 0, :, :, :]) - contract(former[..., 1, :, :, :], latter[..., 1, :, :, :])
    imag_part = contract(former[..., 0, :, :, :], latter[..., 1, :, :, :]) + contract(former[..., 1, :, :, :], latter[..., 0, :, :, :])
    return jnp.stack([real_part, imag_part], axis=-4)

def dyson_update(bare_phonon, prior_polar):
    return bare_phonon + complex_product(complex_product(bare_phonon, prior_polar), bare_phonon)

def flipped_products(blocks, derivative):
    flipped = jnp.einsum('ktcbx,ixa->kticab', blocks.astype(jnp.float32), derivative.astype(jnp.float32))
    sign_flip = jnp.array([1.0, -1.0], jnp.float32).reshape(1, 1, 1, 2, 1, 1)
    return (flipped * sign_flip).astype(jnp.bfloat16)

def mode_weights(chosen):
    real_part = chosen[:, :, 0]
    imag_part = chosen[:, :, 1]
    upper_part = jnp.stack([real_part, -imag_part], axis=2)
    lower_part = jnp.stack([imag_part, real_part], axis=2)
    return jnp.stack([upper_part, lower_part], axis=2)

def reference(green_blocks, derivative, bare_phonon, prior_polar, offsets, momenta):
    phonon = dyson_update(bare_phonon, prior_polar)
    phonon_table = jnp.transpose(phonon, (1, 0, 2, 3, 4, 5))
    flipped = flipped_products(green_blocks, derivative)
    momentum_ids = lax.broadcasted_iota(jnp.int32, (NK, NK), 1)

    def one_point(totals, source_index):
        sigma_sum, polar_sum = totals
        source = lax.dynamic_index_in_dim(green_blocks, source_index, 0, keepdims=False)
        column = lax.dynamic_index_in_dim(momenta, source_index, 1, keepdims=False)
        onehot = (column[:, None] == momentum_ids).astype(jnp.float32)
        chosen = jnp.einsum('kq,qmxija->kmxija', onehot, phonon_table, precision=lax.Precision.HIGHEST)
        blocks = jnp.einsum('iab,scbd->iscad', derivative.astype(jnp.float32), source.astype(jnp.float32)).astype(jnp.bfloat16)
        padded = jnp.pad(blocks, ((0, 0), (E_DEV, 0), (0, 0), (0, 0), (0, 0)))
        selected = jnp.stack([lax.dynamic_slice_in_dim(padded, E_DEV - offsets[mode_index], NE, 1) for mode_index in range(NW)], axis=2)
        weights = mode_weights(chosen)
        combined = jnp.einsum('kmxyija,itmyab->ktjxab', weights, selected.astype(jnp.float32), precision=lax.Precision.HIGHEST).astype(jnp.bfloat16)
        sigma_part = jnp.einsum('ktjxab,jbd->ktxad', combined.astype(jnp.float32), derivative.astype(jnp.float32))
        polar_part = jnp.einsum('itmcab,kticab->kmia', selected.astype(jnp.float32), flipped.astype(jnp.float32))
        polar_sum = polar_sum + jnp.einsum('kq,kmia->qmia', onehot, polar_part, precision=lax.Precision.HIGHEST)
        return ((sigma_sum + sigma_part, polar_sum), None)
    initial = (jnp.zeros((NK, NE, 2, NB, NB), jnp.float32), jnp.zeros((NK, NW, 3, NB), jnp.float32))
    (sigma_sum, polar_sum), _ = lax.scan(one_point, initial, jnp.arange(NK, dtype=jnp.int32))
    sigma_scale = 1.0 / math.sqrt(9.0 * NW * NK)
    polar_scale = 1.0 / math.sqrt(float(NK * NE * NB))
    polarization = jnp.transpose(polar_sum, (1, 0, 2, 3)) * polar_scale
    return (sigma_sum * sigma_scale, polarization)
```

```python
import math

import jax
import jax.numpy as jnp
from jax import lax
from jax.experimental import pallas as pl
from jax.experimental.pallas import tpu as pltpu
from jax.sharding import PartitionSpec as P


NB = 128
BLK = 4 * NB
PH = 32
SHIFTS = [(dx, dy) for dx in range(4) for dy in range(2)]
OFFS = 2

VMEM = pl.BlockSpec(memory_space=pltpu.VMEM)
SMEM = pl.BlockSpec(memory_space=pltpu.SMEM)


def mom_pairs(dx, dy):
    return [(2 * x + y, 2 * ((x + dx) % 4) + (y ^ dy)) for x in range(4) for y in range(2)]


def cmul(former, latter):
    out = []
    for i in range(3):
        row = []
        for j in range(3):
            real = imag = None
            for m in range(3):
                fr, fi = former[i][m]
                lr, li = latter[m][j]
                rr = fr * lr - fi * li
                ii = fr * li + fi * lr
                real = rr if real is None else real + rr
                imag = ii if imag is None else imag + ii
            row.append((real, imag))
        out.append(row)
    return out


def prep_kernel(green_ref, bare_ref, prior_ref, payload_ref, rows_ref):
    for t in range(4):
        payload_ref[t * NB : (t + 1) * NB, :] = green_ref[t].T

    def entries(ref):
        return [[(ref[i, j, 0:1, :], ref[i, j, 1:2, :]) for j in range(3)] for i in range(3)]

    bare = entries(bare_ref)
    change = cmul(cmul(bare, entries(prior_ref)), bare)
    rows_ref[...] = jnp.zeros((PH, NB), jnp.float32)
    for x in range(2):
        for i in range(3):
            for j in range(3):
                at = x * 9 + i * 3 + j
                rows_ref[at : at + 1, :] = bare[i][j][x] + change[i][j][x]
    payload_ref[BLK : BLK + PH, :] = rows_ref[...].astype(jnp.bfloat16)


def side_by_side(deriv_ref):
    plain = jnp.concatenate([deriv_ref[i] for i in range(3)], axis=1)
    turned = jnp.concatenate([deriv_ref[i].T for i in range(3)], axis=1)
    return plain, turned


def place():
    me = lax.axis_index("mom")
    return me, me // 2, me % 2


def polar_rows(scale, which, mom_ref, deriv_ref, along_ref, across_ref, own, slots, out_ref, x_ref):
    plain, turned = side_by_side(deriv_ref)
    me, mx, my = place()
    last = lax.axis_index("en") == 7

    def target(e, x):
        rows = slice((e % 2 * 2 + x) * NB, (e % 2 * 2 + x + 1) * NB)
        block = own[rows, :] if e < 2 else jnp.where(last, across_ref[rows, :], along_ref[rows, :])
        return -block if x else block

    left = jnp.concatenate(
        [
            jnp.concatenate([target(e + off, x) for e in range(2) for x in range(2)], axis=1)
            for off in (1, 2)
        ],
        axis=0,
    )
    for n in range(len(which)):
        x_ref[n * 2 * NB : (n + 1) * 2 * NB, :] = jnp.dot(
            left, slots[n][:BLK, :], preferred_element_type=jnp.float32
        ).astype(jnp.bfloat16)
    plain32 = plain.astype(jnp.float32) * scale
    for n, s in enumerate(which):
        dx, dy = SHIFTS[s]
        z = jnp.dot(
            x_ref[n * 2 * NB : (n + 1) * 2 * NB, :], turned, preferred_element_type=jnp.float32
        )
        source = 2 * ((mx + 4 - dx) % 4) + (my + dy) % 2
        q = mom_ref[me, source]
        for off in range(OFFS):
            row = jnp.sum(z[off * NB : (off + 1) * NB, :] * plain32, axis=0, keepdims=True)
            for i in range(3):
                at = off * 3 + i
                out_ref[q, at : at + 1, :] = row[:, i * NB : (i + 1) * NB]


def early_kernel(scale, which, mom_ref, deriv_ref, along_ref, across_ref, *refs):
    slots, (out_ref, x_ref) = refs[: len(which)], refs[len(which) :]
    out_ref[...] = jnp.zeros(out_ref.shape, jnp.float32)
    polar_rows(scale, which, mom_ref, deriv_ref, along_ref, across_ref, slots[0], slots, out_ref, x_ref)


def late_kernel(scale, which, mom_ref, deriv_ref, along_ref, across_ref, sofar_ref, *refs):
    slots, (out_ref, phonon_ref, x_ref) = refs[:8], refs[8:]
    out_ref[...] = sofar_ref[...]
    for s in range(8):
        phonon_ref[s] = slots[s][BLK:, :]
    late = [slots[s] for s in which]
    polar_rows(scale, which, mom_ref, deriv_ref, along_ref, across_ref, slots[0], late, out_ref, x_ref)


def sigma_kernel(scale, mom_ref, off_ref, deriv_ref, *refs):
    slots = refs[:8]
    modes = refs[8:12]
    own_ref, rim_ref, w_ref, m_ref, acc_ref = refs[12:]
    _, turned = side_by_side(deriv_ref)
    me, mx, my = place()
    sec = lax.axis_index("sec")
    for off in range(OFFS):
        total = None
        for d in range(4):
            on = (off_ref[sec ^ d] == off + 1).astype(jnp.float32)
            term = modes[d][...].astype(jnp.float32) * on
            total = term if total is None else total + term
        w_ref[:, off] = total
    turned32 = turned.astype(jnp.float32)
    for s, (dx, dy) in enumerate(SHIFTS):
        source = 2 * ((mx + 4 - dx) % 4) + (my + dy) % 2
        q = mom_ref[me, source]
        at_slot = 2 * ((mx + 4 - q // 2) % 4) + (my + q) % 2
        for off in range(OFFS):
            w = w_ref[at_slot, off]
            for j in range(3):
                for x in range(2):
                    total = None
                    for i in range(3):
                        r = x * 9 + i * 3 + j
                        term = w[r : r + 1, :] * turned32[:, i * NB : (i + 1) * NB]
                        total = term if total is None else total + term
                    col = ((off * 3 + j) * 2 + x) * NB
                    m_ref[s * NB : (s + 1) * NB, col : col + NB] = total.astype(jnp.bfloat16)
        if s % 2 == 1:
            left = jnp.concatenate([slots[s - 1][:BLK, :], slots[s][:BLK, :]], axis=1)
            part = jnp.dot(
                left, m_ref[(s - 1) * NB : (s + 1) * NB, :], preferred_element_type=jnp.float32
            )
            if s == 1:
                acc_ref[...] = part
            else:
                acc_ref[...] += part

    def piece(e, y, off, j, x):
        col = ((off * 3 + j) * 2 + x) * NB
        row = (e * 2 + y) * NB
        return acc_ref[row : row + NB, col : col + NB]

    def combined(e, off, j):
        real = piece(e, 0, off, j, 0) - piece(e, 1, off, j, 1)
        imag = piece(e, 0, off, j, 1) + piece(e, 1, off, j, 0)
        return real, imag

    rows = []
    for j in range(3):
        a, b, c, d = combined(0, 0, j), combined(0, 1, j), combined(1, 0, j), combined(1, 1, j)
        rows.append(
            jnp.concatenate([a[0], a[1], b[0] + c[0], b[1] + c[1], d[0], d[1]], axis=1).astype(
                jnp.bfloat16
            )
        )
    right = jnp.concatenate(rows, axis=0)
    result = jnp.dot(turned, right, preferred_element_type=jnp.float32) * scale
    for x in range(2):
        own_ref[0, x] = jnp.zeros((NB, NB), jnp.float32)
        own_ref[1, x] = result[:, x * NB : (x + 1) * NB].T
    for t in range(4):
        col = (2 + t) * NB
        rim_ref[t // 2, t % 2] = result[:, col : col + NB].T.astype(jnp.bfloat16)


def finish_kernel(off_ref, parts_ref, out_ref):
    total = jnp.sum(parts_ref[...], axis=0)
    first = (off_ref[lax.axis_index("sec")] == 1).astype(jnp.float32)
    for i in range(3):
        out_ref[i] = total[i : i + 1] * first + total[3 + i : 4 + i] * (1.0 - first)


EARLY = (0, 1, 2, 6, 4)
LATE = (3, 7, 5)


def per_device(green_blocks, derivative, bare_phonon, prior_polar, offsets, momenta):
    levels = 64
    polar_scale = 1.0 / math.sqrt(8.0 * levels * NB)
    sigma_scale = 1.0 / math.sqrt(9.0 * 4 * 8)
    payload = pl.pallas_call(
        prep_kernel,
        out_shape=jax.ShapeDtypeStruct((BLK + PH, NB), jnp.bfloat16),
        in_specs=[VMEM] * 3,
        out_specs=VMEM,
        scratch_shapes=[pltpu.VMEM((PH, NB), jnp.float32)],
        name="prep",
    )(
        green_blocks.reshape(4, NB, NB),
        jnp.transpose(bare_phonon, (0, 1, 3, 4, 2, 5)).reshape(3, 3, 2, NB),
        jnp.transpose(prior_polar, (0, 1, 3, 4, 2, 5)).reshape(3, 3, 2, NB),
    )
    slots = [payload] + [None] * 7

    for s in (1, 2, 6, 4):
        slots[s] = lax.ppermute(payload, "mom", mom_pairs(*SHIFTS[s]))
    along = lax.ppermute(payload, "en", [(i, (i - 1) % 8) for i in range(8)])
    for s in (5, 3, 7):
        slots[s] = lax.ppermute(slots[1], "mom", mom_pairs(SHIFTS[s][0], 0))
    across = lax.ppermute(along, ("sec", "en"), [(8 * i + 15, 8 * i + 7) for i in range(3)])
    sofar = pl.pallas_call(
        lambda *refs: early_kernel(polar_scale, EARLY, *refs),
        out_shape=jax.ShapeDtypeStruct((8, 8, NB), jnp.float32),
        in_specs=[SMEM] + [VMEM] * (3 + len(EARLY)),
        out_specs=VMEM,
        scratch_shapes=[pltpu.VMEM((len(EARLY) * 2 * NB, NB), jnp.bfloat16)],
        cost_estimate=pl.CostEstimate(
            flops=1000000000, bytes_accessed=1000000, transcendentals=0
        ),
        name="early",
        compiler_params=pltpu.CompilerParams(vmem_limit_bytes=6 * 2**20),
    )(momenta, derivative, along, across, *[slots[s] for s in EARLY])
    polar, phonon = pl.pallas_call(
        lambda *refs: late_kernel(polar_scale, LATE, *refs),
        out_shape=(
            jax.ShapeDtypeStruct((8, 8, NB), jnp.float32),
            jax.ShapeDtypeStruct((8, PH, NB), jnp.bfloat16),
        ),
        in_specs=[SMEM] + [VMEM] * 12,
        out_specs=(VMEM, VMEM),
        scratch_shapes=[pltpu.VMEM((len(LATE) * 2 * NB, NB), jnp.bfloat16)],
        name="late",
        compiler_params=pltpu.CompilerParams(vmem_limit_bytes=6 * 2**20),
    )(momenta, derivative, along, across, sofar, *slots)
    by_point = lax.all_to_all(polar, "mom", 0, 0, tiled=True)
    modes = [phonon] + [
        lax.ppermute(phonon, "sec", [(i, i ^ d) for i in range(4)]) for d in (1, 2, 3)
    ]
    own, rim = pl.pallas_call(
        lambda *refs: sigma_kernel(sigma_scale, *refs),
        out_shape=(
            jax.ShapeDtypeStruct((2, 2, NB, NB), jnp.float32),
            jax.ShapeDtypeStruct((2, 2, NB, NB), jnp.bfloat16),
        ),
        in_specs=[SMEM, SMEM] + [VMEM] * 13,
        out_specs=(VMEM, VMEM),
        scratch_shapes=[
            pltpu.VMEM((8, OFFS, PH, NB), jnp.float32),
            pltpu.VMEM((8 * NB, 12 * NB), jnp.bfloat16),
            pltpu.VMEM((BLK, 12 * NB), jnp.float32),
        ],
        cost_estimate=pl.CostEstimate(flops=2000000000, bytes_accessed=2000000, transcendentals=0),
        name="sigma",
        compiler_params=pltpu.CompilerParams(vmem_limit_bytes=16 * 2**20),
    )(momenta, offsets, derivative, *slots, *modes)
    up = lax.ppermute(rim, "en", [(i, (i + 1) % 8) for i in range(8)])
    over = lax.ppermute(up, ("sec", "en"), [(8 * i, 8 * i + 8) for i in range(3)])
    mine = jnp.sum(by_point, axis=0)
    copies = jnp.broadcast_to(mine[None], (32,) + mine.shape)
    spread = lax.all_to_all(copies, ("sec", "en"), 0, 0, tiled=True)
    below = jnp.where(lax.axis_index("en") == 0, over, up)
    sigma = own + below.astype(jnp.float32)
    spread, sigma = lax.optimization_barrier((spread, sigma))
    polarization = pl.pallas_call(
        finish_kernel,
        out_shape=jax.ShapeDtypeStruct((3, 1, NB), jnp.float32),
        in_specs=[SMEM, VMEM],
        out_specs=VMEM,
        name="finish",
        compiler_params=pltpu.CompilerParams(vmem_limit_bytes=2 * 2**20),
    )(offsets, spread)
    polarization = jnp.transpose(polarization.reshape(1, 3, 1, NB), (0, 2, 1, 3))
    return sigma[None], polarization


def solution(mesh):
    return jax.shard_map(
        per_device,
        mesh=mesh,
        in_specs=(
            P("mom", ("sec", "en"), None, None, None),
            P(),
            P("sec", "mom", None, None, None, None),
            P("sec", "mom", None, None, None, None),
            P(),
            P(),
        ),
        out_specs=(P("mom", ("sec", "en"), None, None, None), P("sec", "mom", None, None)),
        check_vma=False,
    )
```

```python
import math

import jax
import jax.numpy as jnp
from jax import lax
from jax.experimental import pallas as pl
from jax.experimental.pallas import tpu as pltpu
from jax.sharding import PartitionSpec as P


NB = 128
BLK = 4 * NB
PH = 32
SHIFTS = [(dx, dy) for dx in range(4) for dy in range(2)]
OFFS = 2

VMEM = pl.BlockSpec(memory_space=pltpu.VMEM)
SMEM = pl.BlockSpec(memory_space=pltpu.SMEM)


def mom_pairs(dx, dy):
    return [(2 * x + y, 2 * ((x + dx) % 4) + (y ^ dy)) for x in range(4) for y in range(2)]


def cmul(former, latter):
    out = []
    for i in range(3):
        row = []
        for j in range(3):
            real = imag = None
            for m in range(3):
                fr, fi = former[i][m]
                lr, li = latter[m][j]
                rr = fr * lr - fi * li
                ii = fr * li + fi * lr
                real = rr if real is None else real + rr
                imag = ii if imag is None else imag + ii
            row.append((real, imag))
        out.append(row)
    return out


def prep_kernel(green_ref, bare_ref, prior_ref, payload_ref, rows_ref):
    for t in range(4):
        payload_ref[t * NB : (t + 1) * NB, :] = green_ref[t].T

    def entries(ref):
        return [[(ref[i, j, 0:1, :], ref[i, j, 1:2, :]) for j in range(3)] for i in range(3)]

    bare = entries(bare_ref)
    change = cmul(cmul(bare, entries(prior_ref)), bare)
    rows_ref[...] = jnp.zeros((PH, NB), jnp.float32)
    for x in range(2):
        for i in range(3):
            for j in range(3):
                at = x * 9 + i * 3 + j
                rows_ref[at : at + 1, :] = bare[i][j][x] + change[i][j][x]
    payload_ref[BLK : BLK + PH, :] = rows_ref[...].astype(jnp.bfloat16)


def side_by_side(deriv_ref):
    plain = jnp.concatenate([deriv_ref[i] for i in range(3)], axis=1)
    turned = jnp.concatenate([deriv_ref[i].T for i in range(3)], axis=1)
    return plain, turned


def place():
    me = lax.axis_index("mom")
    return me, me // 2, me % 2


def targets_side(own, along_ref, across_ref):
    last = lax.axis_index("en") == 7

    def target(e, x):
        rows = slice((e % 2 * 2 + x) * NB, (e % 2 * 2 + x + 1) * NB)
        block = own[rows, :] if e < 2 else jnp.where(last, across_ref[rows, :], along_ref[rows, :])
        return -block if x else block

    return jnp.concatenate(
        [
            jnp.concatenate([target(e + off, x) for e in range(2) for x in range(2)], axis=1)
            for off in (1, 2)
        ],
        axis=0,
    )


def polar_rows(which, mom_ref, left, plain32, turned, slots, out_ref, x_ref):
    me, mx, my = place()
    for n in range(len(which)):
        x_ref[n * 2 * NB : (n + 1) * 2 * NB, :] = jnp.dot(
            left, slots[n][:BLK, :], preferred_element_type=jnp.float32
        ).astype(jnp.bfloat16)
    for n, s in enumerate(which):
        dx, dy = SHIFTS[s]
        z = jnp.dot(
            x_ref[n * 2 * NB : (n + 1) * 2 * NB, :], turned, preferred_element_type=jnp.float32
        )
        source = 2 * ((mx + 4 - dx) % 4) + (my + dy) % 2
        q = mom_ref[me, source]
        for off in range(OFFS):
            row = jnp.sum(z[off * NB : (off + 1) * NB, :] * plain32, axis=0, keepdims=True)
            for i in range(3):
                at = off * 3 + i
                out_ref[q, at : at + 1, :] = row[:, i * NB : (i + 1) * NB]


def early_kernel(scale, which, mom_ref, deriv_ref, along_ref, across_ref, *refs):
    slots, (out_ref, left_ref, plain_ref, turned_ref, x_ref) = refs[: len(which)], refs[len(which) :]
    plain, turned = side_by_side(deriv_ref)
    left = targets_side(slots[0], along_ref, across_ref)
    plain32 = plain.astype(jnp.float32) * scale
    left_ref[...] = left
    plain_ref[...] = plain32
    turned_ref[...] = turned
    out_ref[...] = jnp.zeros(out_ref.shape, jnp.float32)
    polar_rows(which, mom_ref, left, plain32, turned, slots, out_ref, x_ref)


def late_kernel(which, mom_ref, sofar_ref, left_ref, plain_ref, turned_ref, *refs):
    slots, (out_ref, phonon_ref, x_ref) = refs[:8], refs[8:]
    out_ref[...] = sofar_ref[...]
    for s in range(8):
        phonon_ref[s] = slots[s][BLK:, :]
    late = [slots[s] for s in which]
    polar_rows(which, mom_ref, left_ref[...], plain_ref[...], turned_ref[...], late, out_ref, x_ref)


def sigma_kernel(scale, mom_ref, off_ref, turned_ref, *refs):
    slots = refs[:8]
    modes = refs[8:12]
    own_ref, rim_ref, w_ref, m_ref, acc_ref = refs[12:]
    turned = turned_ref[...]
    me, mx, my = place()
    sec = lax.axis_index("sec")
    for off in range(OFFS):
        total = None
        for d in range(4):
            on = (off_ref[sec ^ d] == off + 1).astype(jnp.float32)
            term = modes[d][...].astype(jnp.float32) * on
            total = term if total is None else total + term
        w_ref[:, off] = total
    turned32 = turned.astype(jnp.float32)
    for s, (dx, dy) in enumerate(SHIFTS):
        source = 2 * ((mx + 4 - dx) % 4) + (my + dy) % 2
        q = mom_ref[me, source]
        at_slot = 2 * ((mx + 4 - q // 2) % 4) + (my + q) % 2
        for off in range(OFFS):
            w = w_ref[at_slot, off]
            for j in range(3):
                for x in range(2):
                    total = None
                    for i in range(3):
                        r = x * 9 + i * 3 + j
                        term = w[r : r + 1, :] * turned32[:, i * NB : (i + 1) * NB]
                        total = term if total is None else total + term
                    col = ((off * 3 + j) * 2 + x) * NB
                    m_ref[s * NB : (s + 1) * NB, col : col + NB] = total.astype(jnp.bfloat16)
        if s % 2 == 1:
            left = jnp.concatenate([slots[s - 1][:BLK, :], slots[s][:BLK, :]], axis=1)
            part = jnp.dot(
                left, m_ref[(s - 1) * NB : (s + 1) * NB, :], preferred_element_type=jnp.float32
            )
            if s == 1:
                acc_ref[...] = part
            else:
                acc_ref[...] += part

    def piece(e, y, off, j, x):
        col = ((off * 3 + j) * 2 + x) * NB
        row = (e * 2 + y) * NB
        return acc_ref[row : row + NB, col : col + NB]

    def combined(e, off, j):
        real = piece(e, 0, off, j, 0) - piece(e, 1, off, j, 1)
        imag = piece(e, 0, off, j, 1) + piece(e, 1, off, j, 0)
        return real, imag

    rows = []
    for j in range(3):
        a, b, c, d = combined(0, 0, j), combined(0, 1, j), combined(1, 0, j), combined(1, 1, j)
        rows.append(
            jnp.concatenate([a[0], a[1], b[0] + c[0], b[1] + c[1], d[0], d[1]], axis=1).astype(
                jnp.bfloat16
            )
        )
    right = jnp.concatenate(rows, axis=0)
    result = jnp.dot(turned, right, preferred_element_type=jnp.float32) * scale
    for x in range(2):
        own_ref[0, x] = jnp.zeros((NB, NB), jnp.float32)
        own_ref[1, x] = result[:, x * NB : (x + 1) * NB].T
    for t in range(4):
        col = (2 + t) * NB
        rim_ref[t // 2, t % 2] = result[:, col : col + NB].T.astype(jnp.bfloat16)


EARLY = (0, 1, 2, 6, 4)
LATE = (3, 7, 5)


def per_device(green_blocks, derivative, bare_phonon, prior_polar, offsets, momenta):
    levels = 64
    polar_scale = 1.0 / math.sqrt(8.0 * levels * NB)
    sigma_scale = 1.0 / math.sqrt(9.0 * 4 * 8)
    payload = pl.pallas_call(
        prep_kernel,
        out_shape=jax.ShapeDtypeStruct((BLK + PH, NB), jnp.bfloat16),
        in_specs=[VMEM] * 3,
        out_specs=VMEM,
        scratch_shapes=[pltpu.VMEM((PH, NB), jnp.float32)],
        name="prep",
    )(
        green_blocks.reshape(4, NB, NB),
        jnp.transpose(bare_phonon, (0, 1, 3, 4, 2, 5)).reshape(3, 3, 2, NB),
        jnp.transpose(prior_polar, (0, 1, 3, 4, 2, 5)).reshape(3, 3, 2, NB),
    )
    slots = [payload] + [None] * 7

    for s in (1, 2, 6, 4):
        slots[s] = lax.ppermute(payload, "mom", mom_pairs(*SHIFTS[s]))
    along = lax.ppermute(payload, "en", [(i, (i - 1) % 8) for i in range(8)])
    for s in (5, 3, 7):
        slots[s] = lax.ppermute(slots[1], "mom", mom_pairs(SHIFTS[s][0], 0))
    across = lax.ppermute(along, ("sec", "en"), [(8 * i + 15, 8 * i + 7) for i in range(3)])
    sofar, left, plain, turned = pl.pallas_call(
        lambda *refs: early_kernel(polar_scale, EARLY, *refs),
        out_shape=(
            jax.ShapeDtypeStruct((8, 8, NB), jnp.float32),
            jax.ShapeDtypeStruct((2 * NB, BLK), jnp.bfloat16),
            jax.ShapeDtypeStruct((NB, 3 * NB), jnp.float32),
            jax.ShapeDtypeStruct((NB, 3 * NB), jnp.bfloat16),
        ),
        in_specs=[SMEM] + [VMEM] * (3 + len(EARLY)),
        out_specs=(VMEM,) * 4,
        scratch_shapes=[pltpu.VMEM((len(EARLY) * 2 * NB, NB), jnp.bfloat16)],
        cost_estimate=pl.CostEstimate(
            flops=1000000000, bytes_accessed=1000000, transcendentals=0
        ),
        name="early",
        compiler_params=pltpu.CompilerParams(vmem_limit_bytes=6 * 2**20),
    )(momenta, derivative, along, across, *[slots[s] for s in EARLY])
    polar, phonon = pl.pallas_call(
        lambda *refs: late_kernel(LATE, *refs),
        out_shape=(
            jax.ShapeDtypeStruct((8, 8, NB), jnp.float32),
            jax.ShapeDtypeStruct((8, PH, NB), jnp.bfloat16),
        ),
        in_specs=[SMEM] + [VMEM] * 12,
        out_specs=(VMEM, VMEM),
        scratch_shapes=[pltpu.VMEM((len(LATE) * 2 * NB, NB), jnp.bfloat16)],
        name="late",
        compiler_params=pltpu.CompilerParams(vmem_limit_bytes=6 * 2**20),
    )(momenta, sofar, left, plain, turned, *slots)
    by_point = lax.all_to_all(polar, "mom", 0, 0, tiled=True)
    modes = [phonon] + [
        lax.ppermute(phonon, "sec", [(i, i ^ d) for i in range(4)]) for d in (1, 2, 3)
    ]
    own, rim = pl.pallas_call(
        lambda *refs: sigma_kernel(sigma_scale, *refs),
        out_shape=(
            jax.ShapeDtypeStruct((2, 2, NB, NB), jnp.float32),
            jax.ShapeDtypeStruct((2, 2, NB, NB), jnp.bfloat16),
        ),
        in_specs=[SMEM, SMEM] + [VMEM] * 13,
        out_specs=(VMEM, VMEM),
        scratch_shapes=[
            pltpu.VMEM((8, OFFS, PH, NB), jnp.float32),
            pltpu.VMEM((8 * NB, 12 * NB), jnp.bfloat16),
            pltpu.VMEM((BLK, 12 * NB), jnp.float32),
        ],
        cost_estimate=pl.CostEstimate(flops=2000000000, bytes_accessed=2000000, transcendentals=0),
        name="sigma",
        compiler_params=pltpu.CompilerParams(vmem_limit_bytes=16 * 2**20),
    )(momenta, offsets, turned, *slots, *modes)
    up = lax.ppermute(rim, "en", [(i, (i + 1) % 8) for i in range(8)])
    over = lax.ppermute(up, ("sec", "en"), [(8 * i, 8 * i + 8) for i in range(3)])
    mine = jnp.sum(by_point, axis=0)
    copies = jnp.broadcast_to(mine[None], (32,) + mine.shape)
    spread = lax.all_to_all(copies, ("sec", "en"), 0, 0, tiled=True)
    below = jnp.where(lax.axis_index("en") == 0, over, up)
    sigma = own + below.astype(jnp.float32)
    spread, sigma = lax.optimization_barrier((spread, sigma))
    total = jnp.sum(spread, axis=0)
    first = lax.dynamic_index_in_dim(offsets, lax.axis_index("sec"), 0, keepdims=False) == 1
    polarization = jnp.where(first, total[0:3], total[3:6])[None, None]
    return sigma[None], polarization


def solution(mesh):
    return jax.shard_map(
        per_device,
        mesh=mesh,
        in_specs=(
            P("mom", ("sec", "en"), None, None, None),
            P(),
            P("sec", "mom", None, None, None, None),
            P("sec", "mom", None, None, None, None),
            P(),
            P(),
        ),
        out_specs=(P("mom", ("sec", "en"), None, None, None), P("sec", "mom", None, None)),
        check_vma=False,
    )
```

```python
import math

import jax
import jax.numpy as jnp
from jax import lax
from jax.experimental import pallas as pl
from jax.experimental.pallas import tpu as pltpu
from jax.sharding import PartitionSpec as P


NB = 128
BLK = 4 * NB
PH = 32
SHIFTS = [(dx, dy) for dx in range(4) for dy in range(2)]
OFFS = 2

VMEM = pl.BlockSpec(memory_space=pltpu.VMEM)
SMEM = pl.BlockSpec(memory_space=pltpu.SMEM)


def mom_pairs(dx, dy):
    return [(2 * x + y, 2 * ((x + dx) % 4) + (y ^ dy)) for x in range(4) for y in range(2)]


def cmul(former, latter):
    out = []
    for i in range(3):
        row = []
        for j in range(3):
            real = imag = None
            for m in range(3):
                fr, fi = former[i][m]
                lr, li = latter[m][j]
                rr = fr * lr - fi * li
                ii = fr * li + fi * lr
                real = rr if real is None else real + rr
                imag = ii if imag is None else imag + ii
            row.append((real, imag))
        out.append(row)
    return out


def prep_kernel(green_ref, bare_ref, prior_ref, payload_ref, rows_ref):
    for t in range(4):
        payload_ref[t * NB : (t + 1) * NB, :] = green_ref[t].T

    def entries(ref):
        return [[(ref[i, j, 0:1, :], ref[i, j, 1:2, :]) for j in range(3)] for i in range(3)]

    bare = entries(bare_ref)
    change = cmul(cmul(bare, entries(prior_ref)), bare)
    rows_ref[...] = jnp.zeros((PH, NB), jnp.float32)
    for x in range(2):
        for i in range(3):
            for j in range(3):
                at = x * 9 + i * 3 + j
                rows_ref[at : at + 1, :] = bare[i][j][x] + change[i][j][x]
    payload_ref[BLK : BLK + PH, :] = rows_ref[...].astype(jnp.bfloat16)


def side_by_side(deriv_ref):
    plain = jnp.concatenate([deriv_ref[i] for i in range(3)], axis=1)
    turned = jnp.concatenate([deriv_ref[i].T for i in range(3)], axis=1)
    return plain, turned


def place():
    me = lax.axis_index("mom")
    return me, me // 2, me % 2


def targets_side(own, along_ref, across_ref):
    last = lax.axis_index("en") == 7

    def target(e, x):
        rows = slice((e % 2 * 2 + x) * NB, (e % 2 * 2 + x + 1) * NB)
        block = own[rows, :] if e < 2 else jnp.where(last, across_ref[rows, :], along_ref[rows, :])
        return -block if x else block

    return jnp.concatenate(
        [
            jnp.concatenate([target(e + off, x) for e in range(2) for x in range(2)], axis=1)
            for off in (1, 2)
        ],
        axis=0,
    )


def polar_rows(which, mom_ref, left, plain32, turned, slots, out_ref, x_ref):
    me, mx, my = place()
    for n in range(len(which)):
        x_ref[n * 2 * NB : (n + 1) * 2 * NB, :] = jnp.dot(
            left, slots[n][:BLK, :], preferred_element_type=jnp.float32
        ).astype(jnp.bfloat16)
    for n, s in enumerate(which):
        dx, dy = SHIFTS[s]
        z = jnp.dot(
            x_ref[n * 2 * NB : (n + 1) * 2 * NB, :], turned, preferred_element_type=jnp.float32
        )
        source = 2 * ((mx + 4 - dx) % 4) + (my + dy) % 2
        q = mom_ref[me, source]
        for off in range(OFFS):
            row = jnp.sum(z[off * NB : (off + 1) * NB, :] * plain32, axis=0, keepdims=True)
            for i in range(3):
                at = off * 3 + i
                out_ref[q, at : at + 1, :] = row[:, i * NB : (i + 1) * NB]


def early_kernel(scale, which, mom_ref, deriv_ref, along_ref, across_ref, *refs):
    slots, (out_ref, left_ref, plain_ref, turned_ref, x_ref) = refs[: len(which)], refs[len(which) :]
    plain, turned = side_by_side(deriv_ref)
    left = targets_side(slots[0], along_ref, across_ref)
    plain32 = plain.astype(jnp.float32) * scale
    left_ref[...] = left
    plain_ref[...] = plain32
    turned_ref[...] = turned
    out_ref[...] = jnp.zeros(out_ref.shape, jnp.float32)
    polar_rows(which, mom_ref, left, plain32, turned, slots, out_ref, x_ref)


def late_kernel(which, mom_ref, sofar_ref, left_ref, plain_ref, turned_ref, *refs):
    slots, (out_ref, phonon_ref, x_ref) = refs[:8], refs[8:]
    out_ref[...] = sofar_ref[...]
    for s in range(8):
        phonon_ref[s] = slots[s][BLK:, :]
    late = [slots[s] for s in which]
    polar_rows(which, mom_ref, left_ref[...], plain_ref[...], turned_ref[...], late, out_ref, x_ref)


def sigma_kernel(scale, mom_ref, off_ref, turned_ref, *refs):
    slots = refs[:8]
    modes = refs[8:12]
    own_ref, rim_ref, w_ref, m_ref, acc_ref = refs[12:]
    turned = turned_ref[...]
    me, mx, my = place()
    sec = lax.axis_index("sec")
    for off in range(OFFS):
        total = None
        for d in range(4):
            on = (off_ref[sec ^ d] == off + 1).astype(jnp.float32)
            term = modes[d][...].astype(jnp.float32) * on
            total = term if total is None else total + term
        w_ref[:, off] = total
    turned32 = turned.astype(jnp.float32)
    for s, (dx, dy) in enumerate(SHIFTS):
        source = 2 * ((mx + 4 - dx) % 4) + (my + dy) % 2
        q = mom_ref[me, source]
        at_slot = 2 * ((mx + 4 - q // 2) % 4) + (my + q) % 2
        for off in range(OFFS):
            w = w_ref[at_slot, off]
            for j in range(3):
                for x in range(2):
                    total = None
                    for i in range(3):
                        r = x * 9 + i * 3 + j
                        term = w[r : r + 1, :] * turned32[:, i * NB : (i + 1) * NB]
                        total = term if total is None else total + term
                    col = ((off * 3 + j) * 2 + x) * NB
                    m_ref[s * NB : (s + 1) * NB, col : col + NB] = total.astype(jnp.bfloat16)
        if s % 2 == 1:
            left = jnp.concatenate([slots[s - 1][:BLK, :], slots[s][:BLK, :]], axis=1)
            part = jnp.dot(
                left, m_ref[(s - 1) * NB : (s + 1) * NB, :], preferred_element_type=jnp.float32
            )
            if s == 1:
                acc_ref[...] = part
            else:
                acc_ref[...] += part

    def piece(e, y, off, j, x):
        col = ((off * 3 + j) * 2 + x) * NB
        row = (e * 2 + y) * NB
        return acc_ref[row : row + NB, col : col + NB]

    def combined(e, off, j):
        real = piece(e, 0, off, j, 0) - piece(e, 1, off, j, 1)
        imag = piece(e, 0, off, j, 1) + piece(e, 1, off, j, 0)
        return real, imag

    rows = []
    for j in range(3):
        a, b, c, d = combined(0, 0, j), combined(0, 1, j), combined(1, 0, j), combined(1, 1, j)
        rows.append(
            jnp.concatenate([a[0], a[1], b[0] + c[0], b[1] + c[1], d[0], d[1]], axis=1).astype(
                jnp.bfloat16
            )
        )
    right = jnp.concatenate(rows, axis=0)
    result = jnp.dot(turned, right, preferred_element_type=jnp.float32) * scale
    for x in range(2):
        own_ref[0, x] = jnp.zeros((NB, NB), jnp.float32)
        own_ref[1, x] = result[:, x * NB : (x + 1) * NB].T
    for t in range(4):
        col = (2 + t) * NB
        rim_ref[t // 2, t % 2] = result[:, col : col + NB].T.astype(jnp.bfloat16)


EARLY = (0, 1, 2, 6, 4)
LATE = (3, 7, 5)


def per_device(green_blocks, derivative, bare_phonon, prior_polar, offsets, momenta):
    levels = 64
    polar_scale = 1.0 / math.sqrt(8.0 * levels * NB)
    sigma_scale = 1.0 / math.sqrt(9.0 * 4 * 8)
    payload = pl.pallas_call(
        prep_kernel,
        out_shape=jax.ShapeDtypeStruct((BLK + PH, NB), jnp.bfloat16),
        in_specs=[VMEM] * 3,
        out_specs=VMEM,
        scratch_shapes=[pltpu.VMEM((PH, NB), jnp.float32)],
        name="prep",
    )(
        green_blocks.reshape(4, NB, NB),
        jnp.transpose(bare_phonon, (0, 1, 3, 4, 2, 5)).reshape(3, 3, 2, NB),
        jnp.transpose(prior_polar, (0, 1, 3, 4, 2, 5)).reshape(3, 3, 2, NB),
    )
    slots = [payload] + [None] * 7

    for s in (1, 2, 6, 4):
        slots[s] = lax.ppermute(payload, "mom", mom_pairs(*SHIFTS[s]))
    along = lax.ppermute(payload, "en", [(i, (i - 1) % 8) for i in range(8)])
    for s in (5, 3, 7):
        slots[s] = lax.ppermute(slots[1], "mom", mom_pairs(SHIFTS[s][0], 0))
    across = lax.ppermute(along, ("sec", "en"), [(8 * i + 15, 8 * i + 7) for i in range(3)])
    sofar, left, plain, turned = pl.pallas_call(
        lambda *refs: early_kernel(polar_scale, EARLY, *refs),
        out_shape=(
            jax.ShapeDtypeStruct((8, 8, NB), jnp.float32),
            jax.ShapeDtypeStruct((2 * NB, BLK), jnp.bfloat16),
            jax.ShapeDtypeStruct((NB, 3 * NB), jnp.float32),
            jax.ShapeDtypeStruct((NB, 3 * NB), jnp.bfloat16),
        ),
        in_specs=[SMEM] + [VMEM] * (3 + len(EARLY)),
        out_specs=(VMEM,) * 4,
        scratch_shapes=[pltpu.VMEM((len(EARLY) * 2 * NB, NB), jnp.bfloat16)],
        cost_estimate=pl.CostEstimate(
            flops=1000000000, bytes_accessed=1000000, transcendentals=0
        ),
        name="early",
        compiler_params=pltpu.CompilerParams(vmem_limit_bytes=6 * 2**20),
    )(momenta, derivative, along, across, *[slots[s] for s in EARLY])
    polar, phonon = pl.pallas_call(
        lambda *refs: late_kernel(LATE, *refs),
        out_shape=(
            jax.ShapeDtypeStruct((8, 8, NB), jnp.float32),
            jax.ShapeDtypeStruct((8, PH, NB), jnp.bfloat16),
        ),
        in_specs=[SMEM] + [VMEM] * 12,
        out_specs=(VMEM, VMEM),
        scratch_shapes=[pltpu.VMEM((len(LATE) * 2 * NB, NB), jnp.bfloat16)],
        name="late",
        compiler_params=pltpu.CompilerParams(vmem_limit_bytes=6 * 2**20),
    )(momenta, sofar, left, plain, turned, *slots)
    polar = polar + lax.ppermute(polar, "sec", [(i, i ^ 1) for i in range(4)])
    by_point = lax.all_to_all(polar, "mom", 0, 0, tiled=True)
    modes = [phonon] + [
        lax.ppermute(phonon, "sec", [(i, i ^ d) for i in range(4)]) for d in (1, 2, 3)
    ]
    own, rim = pl.pallas_call(
        lambda *refs: sigma_kernel(sigma_scale, *refs),
        out_shape=(
            jax.ShapeDtypeStruct((2, 2, NB, NB), jnp.float32),
            jax.ShapeDtypeStruct((2, 2, NB, NB), jnp.bfloat16),
        ),
        in_specs=[SMEM, SMEM] + [VMEM] * 13,
        out_specs=(VMEM, VMEM),
        scratch_shapes=[
            pltpu.VMEM((8, OFFS, PH, NB), jnp.float32),
            pltpu.VMEM((8 * NB, 12 * NB), jnp.bfloat16),
            pltpu.VMEM((BLK, 12 * NB), jnp.float32),
        ],
        cost_estimate=pl.CostEstimate(flops=2000000000, bytes_accessed=2000000, transcendentals=0),
        name="sigma",
        compiler_params=pltpu.CompilerParams(vmem_limit_bytes=16 * 2**20),
    )(momenta, offsets, turned, *slots, *modes)
    up = lax.ppermute(rim, "en", [(i, (i + 1) % 8) for i in range(8)])
    over = lax.ppermute(up, ("sec", "en"), [(8 * i, 8 * i + 8) for i in range(3)])
    mine = jnp.sum(by_point, axis=0)
    copies = jnp.broadcast_to(mine[None], (16,) + mine.shape)
    groups = [[8 * (core + 2 * far) + e for far in range(2) for e in range(8)] for core in range(2)]
    spread = lax.all_to_all(
        copies, ("sec", "en"), 0, 0, axis_index_groups=groups, tiled=True
    )
    below = jnp.where(lax.axis_index("en") == 0, over, up)
    sigma = own + below.astype(jnp.float32)
    spread, sigma = lax.optimization_barrier((spread, sigma))
    total = jnp.sum(spread, axis=0)
    first = lax.dynamic_index_in_dim(offsets, lax.axis_index("sec"), 0, keepdims=False) == 1
    polarization = jnp.where(first, total[0:3], total[3:6])[None, None]
    return sigma[None], polarization


def solution(mesh):
    return jax.shard_map(
        per_device,
        mesh=mesh,
        in_specs=(
            P("mom", ("sec", "en"), None, None, None),
            P(),
            P("sec", "mom", None, None, None, None),
            P("sec", "mom", None, None, None, None),
            P(),
            P(),
        ),
        out_specs=(P("mom", ("sec", "en"), None, None, None), P("sec", "mom", None, None)),
        check_vma=False,
    )
```
